256 devices in a mesh: dp: 4 (over x_hi, core), latent: 64 (over y, x_lo, z).
Axes of the slice: x: 4 (x_hi: 2, x_lo: 2; x = x_hi * 2 + x_lo), y: 4, z: 8, core: 2. Of those that a mesh axis runs over, the one named last changes fastest.
Arguments:
- activations: bfloat16 [32768, 8192], P(('dp', 'latent')), may hold values from -6 to 6
- owner_ids: int32 [32768, 2], P(('dp', 'latent')), may hold values from 0 to 63, all different within a row; in each aligned block of 128 rows (0 to 127, 128 to 255, ...) at most 6 rows name the same one
- block_mask: int32 [32768, 2, 8], P(('dp', 'latent')), may hold values 0 or 1
- latent_codes: bfloat16 [32768, 2, 1024], P(('dp', 'latent')), may hold values from 0.099609375 to 4
- w_dec: bfloat16 [65536, 8192], P('latent', 'dp'), may hold values from -0.125 to 0.125
- b_dec: float32 [8192], replicated, may hold values from -3 to 3
Outputs:
- rebuilt: bfloat16 [32768, 8192], P(('dp', 'latent'))
- decoder_grad: bfloat16 [65536, 8192], P('latent', 'dp')
The draws below stay inside these ranges and needn't reach their ends.
Inputs may be any that keep to these rules, and one draw needn't show every extreme that they name: `owner_ids`: each row names 2 different owners; among the rows of one device no owner is named more than 6 times, and in every draw some device names some owner exactly 6 times.
All inputs are finite; a program needn't handle non-finite values. No bound on the sum of `block_mask` on one device may be relied on, other than what follows from the above.
Results may differ from the reference program's by a relative error of at most 0.0047.
Values may be sent and summed in bfloat16 or wider, within the bound.
A program may use at most 128 MiB of HBM per device.

```python
import math
import jax
import jax.numpy as jnp
import numpy as np
from jax import lax

D = 8192
BLK = 128
BPO = 8
G = 2
R_DEV = 128
SLAB = 1024
ROWS = 32768
LATENTS = 65536
MOST = 6
N_DP = 4
N_LATENT = 64


def plant(drawn, rng, low, largest):
    shape = drawn.shape
    index_at = [jax.random.randint(jax.random.fold_in(rng, axis), (), 0, shape[axis]) for axis in range(len(shape))]
    drawn = drawn.at[tuple(index_at)].set(low)
    longest = shape.index(max(shape))
    index_at[longest] = (index_at[longest] + 1) % shape[longest]
    return drawn.at[tuple(index_at)].set(largest)


def block_scale(rng, extent, split, smallest, high):
    factor_of = 1.0
    for dim, parts in split:
        heights = jax.random.uniform(jax.random.fold_in(jax.random.fold_in(rng, 6), dim), (parts,), jnp.float32, smallest / len(split), high / len(split))
        factor_of = factor_of * jnp.repeat(jnp.exp(heights), extent[dim] // parts).reshape((-1,) + (1,) * (len(extent) - 1 - dim))
    return factor_of


def shared_out(own_key, own, number, rows, number_of, top, most, skew):
    order = jax.random.permutation(own_key, number_of)
    packed, ordinary = portions_of(number_of, rows * top, most, skew, True), portions_of(number_of, rows * top, most, skew, False)
    places = jnp.arange(number_of)

    def named(lengths, rotation):
        used = int((lengths > 0).sum())
        fixed = max(1, used // 4)
        moved = fixed + (places - fixed + rotation * (used - fixed)) % max(1, number_of - fixed)
        return jnp.zeros((number_of,), jnp.int32).at[order[jnp.where(places < fixed, places, moved)]].set(jnp.asarray(lengths, jnp.int32))

    lengths = jnp.where(number % 4 == 0, named(packed, number // 4), named(ordinary, number - number // 4 - 1))
    mixed = jax.random.permutation(jax.random.fold_in(own, 3), number_of)
    donor, taker = mixed[0:number_of // 2 * 2:2], mixed[1:number_of // 2 * 2:2]
    room = jnp.minimum(lengths[donor] - 1, most - lengths[taker]) // 2
    room = jnp.where((donor == order[0]) | (taker == order[0]) | (lengths[taker] == 0), 0, jnp.maximum(room, 0))
    moved = jax.random.randint(jax.random.fold_in(own, 4), (number_of // 2,), 0, 1 << 20) % (room + 1)
    lengths = lengths.at[donor].add(-moved).at[taker].add(moved)
    labels = jnp.searchsorted(jnp.cumsum(lengths), jnp.arange(rows * top), side="right").astype(jnp.int32)
    grid = labels.reshape(top, rows).T
    grid = grid[jax.random.permutation(jax.random.fold_in(own, 1), rows)]
    rotation = jax.random.randint(jax.random.fold_in(own, 2), (rows, 1), 0, top)
    return jnp.take_along_axis(grid, (jnp.arange(top)[None, :] + rotation) % top, axis=1)


def portions_of(count, total, limit, slope, full):
    weights = [(1 << 20) // math.isqrt(rank ** slope) + 1 for rank in range(1, count + 1)]
    largest = limit if full else min(limit, max(-(-total // count), total * weights[0] // sum(weights)))
    least = 1 if total - largest >= count - 1 else 0
    counts, spare = [largest] + [least] * (count - 1), total - largest - least * (count - 1)
    while spare > 0:
        candidates = [i for i in range(1, count) if counts[i] < largest] or [i for i in range(1, count) if counts[i] < limit]
        mass, budget = sum([weights[i] for i in candidates]), spare
        for i in candidates:
            more = min(limit - counts[i], max(1, budget * weights[i] // mass), spare)
            counts[i] = counts[i] + more
            spare = spare - more
    return np.array(counts)


def scatter_about(key, dims, deviation, bound, pieces=(), kind=jnp.bfloat16):
    drawn = deviation * jax.random.normal(key, dims, jnp.float32)
    if pieces:
        drawn = drawn * block_scale(key, dims, pieces, -0.22, 0.18)
    return jnp.clip(drawn, -bound, bound).astype(kind)


def setup_inputs(seed: int = 0) -> dict:
    key_list = jax.random.split(jax.random.key(seed), 7)
    activations = scatter_about(key_list[0], (ROWS, D), 1.0, 6.0, ((0, 256),))
    owner_ids_keys = jax.random.split(jax.random.fold_in(key_list[1], 1), ROWS // R_DEV)
    owner_ids_turns = jax.random.permutation(jax.random.fold_in(key_list[1], 3), ROWS // R_DEV)
    owner_ids = jax.vmap(lambda own, number: shared_out(jax.random.fold_in(key_list[1], 2), own, number, R_DEV, N_LATENT, G, MOST, 2))(owner_ids_keys, owner_ids_turns).reshape((ROWS, G))
    block_mask = plant((jax.random.randint(key_list[2], (ROWS, G, BPO), 0, 2) < 1).astype(jnp.int32), jax.random.fold_in(key_list[2], 1), 0, 1)
    latent_codes = jnp.clip(jnp.exp(math.log(4.0) - 3.6927934 * jax.random.uniform(key_list[3], (ROWS, G, SLAB), jnp.float32) ** block_scale(key_list[3], (ROWS, G, SLAB), ((0, 256),), -0.2, 0.2)), 0.099609375, 4.0).astype(jnp.bfloat16)
    w_dec = scatter_about(key_list[4], (LATENTS, D), (G * SLAB) ** -0.5, 0.125, ((0, 64), (1, 4)))
    b_dec = scatter_about(key_list[5], (D,), 0.5, 3.0, (), jnp.float32)
    return {"activations": activations, "owner_ids": owner_ids, "block_mask": block_mask, "latent_codes": latent_codes, "w_dec": w_dec, "b_dec": b_dec}


loss_scale = 1.0 / 32.0


def reference(activations, owner_ids, block_mask, latent_codes, w_dec, b_dec):
    slab = BPO * BLK
    visit_count = ROWS * G
    capacity = N_DP * N_LATENT * MOST
    flat_owner = owner_ids.reshape(-1)
    live = block_mask.astype(latent_codes.dtype)[:, :, :, None]
    used = (latent_codes.reshape(ROWS, G, BPO, BLK) * live).reshape(visit_count, slab)
    panels = w_dec.reshape(N_LATENT, slab, D)

    def select(owner):
        hits = flat_owner == owner
        total = jnp.sum(hits.astype(jnp.int32))
        places = jnp.nonzero(hits, size=capacity, fill_value=0)[0].astype(jnp.int32)
        filled = jnp.arange(capacity) < total
        values = jnp.where(filled[:, None], used[places], jnp.zeros((), used.dtype))
        return places // G, values

    def forward(running, owner):
        row_ids, values = select(owner)
        contribution = jnp.dot(values, panels[owner], preferred_element_type=jnp.float32).astype(jnp.bfloat16)
        return running.at[row_ids].add(contribution.astype(jnp.float32)), None

    start_sum = jnp.zeros((ROWS, D), jnp.float32) + b_dec[None, :].astype(jnp.float32)
    rebuilt_wide, _ = lax.scan(forward, start_sum, jnp.arange(N_LATENT))
    rebuilt = rebuilt_wide.astype(jnp.bfloat16)
    errors = (rebuilt_wide - activations.astype(jnp.float32)).astype(jnp.bfloat16)

    def backward(owner):
        row_ids, values = select(owner)
        summed = jnp.dot(values.T, errors[row_ids], preferred_element_type=jnp.float32) * loss_scale
        return summed.astype(jnp.bfloat16)

    gradient = lax.map(backward, jnp.arange(N_LATENT)).reshape(LATENTS, D)
    return rebuilt, gradient
```

```python
import jax
import jax.numpy as jnp
from jax import lax
from jax.sharding import PartitionSpec as P

loss_scale = 1.0 / 32.0
MOST = 6


def on_device(activations, owner_ids, block_mask, latent_codes, w_dec, b_dec):
    row_count, visit_count = owner_ids.shape
    block_count = block_mask.shape[2]
    slab_width = latent_codes.shape[2]
    block_width = slab_width // block_count
    model_width = activations.shape[1]
    owners = lax.axis_size("latent")
    groups = lax.axis_size("dp")
    part_width = model_width // groups
    devices = owners * groups
    slots = owners * MOST
    axes = ("dp", "latent")
    bf16 = jnp.bfloat16

    live = block_mask.astype(bf16)[:, :, :, None]
    used = (latent_codes.reshape(row_count, visit_count, block_count, block_width) * live).reshape(
        row_count, visit_count, slab_width
    )
    same = (owner_ids[:, :, None, None] == owner_ids[None, None, :, :]).astype(jnp.float32)
    row = lax.broadcasted_iota(jnp.int32, (row_count, 1, row_count, 1), 0)
    other = lax.broadcasted_iota(jnp.int32, (row_count, 1, row_count, 1), 2)
    position = jnp.sum(jnp.where(other < row, same, 0.0), axis=(2, 3)).astype(jnp.int32)
    target = owner_ids * MOST + position
    placed = (target[:, :, None] == lax.broadcasted_iota(jnp.int32, (1, 1, slots), 2)).astype(bf16)
    outgoing = jnp.einsum("rgs,rgm->sm", placed, used, preferred_element_type=jnp.float32).astype(bf16)
    outgoing = jnp.broadcast_to(
        outgoing.reshape(1, owners, MOST // 2, 2, slab_width), (groups, owners, MOST // 2, 2, slab_width)
    ).reshape(devices, MOST // 2, 2, slab_width)
    arrived = lax.all_to_all(outgoing, axes, split_axis=0, concat_axis=0, tiled=True)
    arrived = arrived.reshape(devices * MOST, slab_width)
    decoded = jnp.dot(arrived, w_dec, preferred_element_type=jnp.float32).astype(bf16)
    returned = lax.all_to_all(
        decoded.reshape(devices, MOST // 2, 2, part_width), axes, split_axis=0, concat_axis=0, tiled=True
    ).reshape(groups, slots, part_width)
    select = placed[:, 0] + placed[:, 1]
    summed = jnp.einsum("rs,dsj->rdj", select, returned, preferred_element_type=jnp.float32)
    rebuilt_wide = b_dec[None, :] + summed.reshape(row_count, model_width)
    errors = (rebuilt_wide - activations.astype(jnp.float32)).astype(bf16)
    error_slots = jnp.einsum(
        "rs,rdj->dsj", select, errors.reshape(row_count, groups, part_width), preferred_element_type=jnp.float32
    ).astype(bf16)
    error_parts = lax.all_to_all(
        error_slots.reshape(devices, MOST // 2, 2, part_width), axes, split_axis=0, concat_axis=0, tiled=True
    ).reshape(devices * MOST, part_width)
    gradient = (
        lax.dot_general(arrived, error_parts, (((0,), (0,)), ((), ())), preferred_element_type=jnp.float32)
        * loss_scale
    )
    return (rebuilt_wide.astype(bf16), gradient.astype(bf16))


def solution(mesh):
    placed = (
        P(("dp", "latent"), None),
        P(("dp", "latent"), None),
        P(("dp", "latent"), None, None),
        P(("dp", "latent"), None, None),
        P("latent", "dp"),
        P(),
    )
    return jax.shard_map(
        on_device,
        mesh=mesh,
        in_specs=placed,
        out_specs=(P(("dp", "latent"), None), P("latent", "dp")),
        check_vma=False,
    )
```

```python
import jax
import jax.numpy as jnp
from jax import lax
from jax.experimental import pallas as pl
from jax.experimental.pallas import tpu as pltpu
from jax.sharding import PartitionSpec as P

loss_scale = 1.0 / 32.0
MOST = 6


def exchange_kernel(x_ref, o_ref, send_sem, recv_sem, own_sem):
    dp = lax.axis_index("dp")
    latent = lax.axis_index("latent")
    own = pltpu.make_async_copy(x_ref.at[dp * 64 + latent], o_ref.at[dp * 64 + latent], own_sem)
    own.start()

    def step(k, carry):
        ko = k % 64
        to_dp = (dp + k // 64) % 4
        to_latent = ((latent // 16 + ko // 16) % 4) * 16 + ((latent // 8 + ko // 8) % 2) * 8 + (latent + ko) % 8
        pltpu.make_async_remote_copy(
            x_ref.at[to_dp * 64 + to_latent],
            o_ref.at[dp * 64 + latent],
            send_sem,
            recv_sem,
            device_id=(to_dp, to_latent),
            device_id_type=pl.DeviceIdType.MESH,
        ).start()
        return carry

    lax.fori_loop(1, 256, step, 0)
    own.wait()
    rest = o_ref.at[pl.ds(0, 255)]
    pltpu.make_async_copy(rest, rest, send_sem).wait()
    pltpu.make_async_copy(rest, rest, recv_sem).wait()


def exchange(x):
    return pl.pallas_call(
        exchange_kernel,
        out_shape=jax.ShapeDtypeStruct(x.shape, x.dtype),
        in_specs=[pl.BlockSpec(memory_space=pl.ANY)],
        out_specs=pl.BlockSpec(memory_space=pl.ANY),
        scratch_shapes=[pltpu.SemaphoreType.DMA] * 3,
        compiler_params=pltpu.CompilerParams(has_side_effects=True),
    )(x)


def on_device(activations, owner_ids, block_mask, latent_codes, w_dec, b_dec):
    row_count, visit_count = owner_ids.shape
    block_count = block_mask.shape[2]
    slab_width = latent_codes.shape[2]
    block_width = slab_width // block_count
    model_width = activations.shape[1]
    owners = lax.axis_size("latent")
    groups = lax.axis_size("dp")
    part_width = model_width // groups
    devices = owners * groups
    slots = owners * MOST
    axes = ("dp", "latent")
    bf16 = jnp.bfloat16

    live = block_mask.astype(bf16)[:, :, :, None]
    used = (latent_codes.reshape(row_count, visit_count, block_count, block_width) * live).reshape(
        row_count, visit_count, slab_width
    )
    same = (owner_ids[:, :, None, None] == owner_ids[None, None, :, :]).astype(jnp.float32)
    row = lax.broadcasted_iota(jnp.int32, (row_count, 1, row_count, 1), 0)
    other = lax.broadcasted_iota(jnp.int32, (row_count, 1, row_count, 1), 2)
    position = jnp.sum(jnp.where(other < row, same, 0.0), axis=(2, 3)).astype(jnp.int32)
    target = owner_ids * MOST + position
    placed = (target[:, :, None] == lax.broadcasted_iota(jnp.int32, (1, 1, slots), 2)).astype(bf16)
    outgoing = jnp.einsum("rgs,rgm->sm", placed, used, preferred_element_type=jnp.float32).astype(bf16)
    arrived = lax.all_to_all(
        outgoing.reshape(owners, MOST // 2, 2, slab_width), "latent", split_axis=0, concat_axis=0, tiled=True
    )
    arrived = lax.all_gather(arrived, "dp", axis=0, tiled=True)
    arrived = arrived.reshape(devices * MOST, slab_width)
    decoded = jnp.dot(arrived, w_dec, preferred_element_type=jnp.float32).astype(bf16)
    returned = exchange(decoded.reshape(devices, MOST // 2, 2, part_width)).reshape(groups, slots, part_width)
    select = placed[:, 0] + placed[:, 1]
    summed = jnp.einsum("rs,dsj->rdj", select, returned, preferred_element_type=jnp.float32)
    rebuilt_wide = b_dec[None, :] + summed.reshape(row_count, model_width)
    errors = (rebuilt_wide - activations.astype(jnp.float32)).astype(bf16)
    error_slots = jnp.einsum(
        "rs,rdj->dsj", select, errors.reshape(row_count, groups, part_width), preferred_element_type=jnp.float32
    ).astype(bf16)
    error_parts = lax.all_to_all(
        error_slots.reshape(devices, MOST // 2, 2, part_width), axes, split_axis=0, concat_axis=0, tiled=True
    ).reshape(devices * MOST, part_width)
    gradient = (
        lax.dot_general(arrived, error_parts, (((0,), (0,)), ((), ())), preferred_element_type=jnp.float32)
        * loss_scale
    )
    return (rebuilt_wide.astype(bf16), gradient.astype(bf16))


def solution(mesh):
    placed = (
        P(("dp", "latent"), None),
        P(("dp", "latent"), None),
        P(("dp", "latent"), None, None),
        P(("dp", "latent"), None, None),
        P("latent", "dp"),
        P(),
    )
    return jax.shard_map(
        on_device,
        mesh=mesh,
        in_specs=placed,
        out_specs=(P(("dp", "latent"), None), P("latent", "dp")),
        check_vma=False,
    )
```

```python
import jax
import jax.numpy as jnp
import numpy as np
from jax import lax
from jax.experimental import pallas as pl
from jax.experimental.pallas import tpu as pltpu
from jax.sharding import PartitionSpec as P

loss_scale = 1.0 / 32.0
MOST = 6
PAD = 8
PEERS = 8
PARTS = 8
GROUPS = 4
OWNERS = 64
HALF = OWNERS // 2
RUNS = OWNERS // PEERS
BATCH = PEERS * PAD
STACK = PARTS * BATCH
SENT = PARTS * MOST
BF16, F32 = jnp.bfloat16, jnp.float32
MESH = pl.DeviceIdType.MESH


def message_order():
    out = np.zeros((PARTS, PEERS, PAD, PEERS, PARTS, MOST), np.float32)
    for part in range(PARTS):
        for peer in range(PEERS):
            for slot in range(MOST):
                out[part, peer, slot, peer, part, slot] = 1
    return out.reshape(STACK, PEERS * SENT)


def dot(a, b):
    return jnp.dot(a, b, preferred_element_type=F32)


def shifted(latent, offset, sign):
    y = (latent // 16 + sign * (offset // 16) + 4) % 4
    x = (latent // 8 + offset // 8) % 2
    z = (latent % 8 + sign * (offset % 8) + 8) % 8
    return y * 16 + x * 8 + z


def bytes_wait(ref, sem):
    pltpu.make_async_copy(ref, ref, sem).wait()


def kernel(
    rel_ref, mask_ref, codes_ref, bias_ref, spread_ref, pack_ref, act_hbm, w_hbm,
    rebuilt_hbm, grad_hbm,
    w_ref, act_ref, rebuilt_ref, take_ref, put_ref, codes_out, codes_in, codes_t, codes_rows,
    code_tmp, term_tmp, sent, terms_in, errors_in, wide_tmp, error_tmp, error_rows, total, stage,
    load_sem, own_sem, code_send, code_recv, copy_send, copy_recv, term_send, term_recv,
    error_send, error_recv, rebuilt_sem, stage_sem,
):
    dp = lax.axis_index("dp")
    latent = lax.axis_index("latent")
    rows = act_ref.shape[0]
    load_w = pltpu.make_async_copy(w_hbm, w_ref, load_sem.at[0])
    load_act = pltpu.make_async_copy(act_hbm, act_ref, load_sem.at[1])
    load_w.start()
    load_act.start()

    down = lax.broadcasted_iota(jnp.int32, (rows, rows), 0)
    across = lax.broadcasted_iota(jnp.int32, (rows, rows), 1)
    along = [jnp.broadcast_to(rel_ref[g : g + 1, :], (rows, rows)) for g in range(2)]
    below = [jnp.transpose(a) for a in along]
    slot_lane = lax.broadcasted_iota(jnp.int32, (rows, OWNERS * PAD), 1).astype(F32)
    slot_row = lax.broadcasted_iota(jnp.int32, (OWNERS * PAD, rows), 0).astype(F32)
    take = jnp.zeros((rows, OWNERS * PAD), F32)
    puts = []
    for g in range(2):
        count = [jnp.where(below[g] == along[o], 1.0, 0.0) for o in range(2)]
        here = below[g][:, :1] + jnp.sum(jnp.where(across < down, count[0] + count[1], 0.0), axis=1, keepdims=True)
        take = take + jnp.where(slot_lane == here, 1.0, 0.0)
        count = [jnp.where(below[o] == along[g], 1.0, 0.0) for o in range(2)]
        here = rel_ref[g : g + 1, :] + jnp.sum(jnp.where(down < across, count[0] + count[1], 0.0), axis=0, keepdims=True)
        puts.append(jnp.where(slot_row == here, 1.0, 0.0))
    take_ref[...] = take.astype(BF16)
    put_ref[...] = (puts[0] + puts[1]).astype(BF16)
    width = codes_ref.shape[1] // 2
    block = width // PARTS
    for part in range(PARTS):
        placed = jnp.zeros((OWNERS * PAD, block), F32)
        for g in range(2):
            live = mask_ref[g, part : part + 1, :].astype(F32)
            start = g * width + part * block
            placed = placed + dot((puts[g] * live).astype(BF16), codes_ref[:, start : start + block])
        code_tmp[:, part] = placed.astype(BF16).reshape(RUNS, BATCH, block)

    def send_codes(run, carry):
        message = dot(pack_ref[...], code_tmp[run].reshape(STACK, block)).astype(BF16)
        codes_out[pl.ds(run * PEERS, PEERS)] = message.reshape(PEERS, SENT, block)

        def one(i, c):
            ko = run * PEERS + i
            pltpu.make_async_remote_copy(
                codes_out.at[ko], codes_in.at[0, ko], code_send, code_recv.at[run // (RUNS // 2)],
                device_id=(dp, shifted(latent, ko, 1)), device_id_type=MESH,
            ).start()
            return c

        lax.fori_loop(jnp.where(run == 0, 1, 0), PEERS, one, 0)
        return carry

    lax.fori_loop(0, RUNS, send_codes, 0)
    own = pltpu.make_async_copy(codes_out.at[0], codes_in.at[0, 0], own_sem.at[0])
    own.start()
    own.wait()
    unit = lax.broadcasted_iota(jnp.int32, (block, block), 0) == lax.broadcasted_iota(jnp.int32, (block, block), 1)
    unit = jnp.where(unit, 1.0, 0.0).astype(BF16)
    columns = w_ref.shape[1] // PARTS

    def forward(kd, half):
        def spread(g, carry):
            got = codes_in[kd, pl.ds(half * HALF + g * PEERS, PEERS)].reshape(PEERS * SENT, block)
            flat = dot(spread_ref[...], got).astype(BF16)
            for part in range(PARTS):
                codes_rows[pl.ds(g * BATCH, BATCH), part * block : (part + 1) * block] = flat[
                    part * BATCH : (part + 1) * BATCH
                ]
            return carry

        lax.fori_loop(0, RUNS // 2, spread, 0)

        def decode(n, carry):
            at = pl.ds(pl.multiple_of(n * columns, columns), columns)
            term = dot(codes_rows[...], w_ref[:, at]).astype(BF16)
            term_tmp[:, n] = term.reshape(RUNS // 2, BATCH, columns)
            return carry

        lax.fori_loop(0, PARTS, decode, 0)

        def pack(g, carry):
            run = half * (RUNS // 2) + g
            message = dot(pack_ref[...], term_tmp[g].reshape(STACK, columns)).astype(BF16)
            sent[kd, pl.ds(run * PEERS, PEERS)] = message.reshape(PEERS, SENT, columns)

            def one(i, c):
                ko = run * PEERS + i
                pltpu.make_async_remote_copy(
                    sent.at[kd, ko], terms_in.at[kd, ko], term_send.at[kd], term_recv.at[kd],
                    device_id=((dp - kd + GROUPS) % GROUPS, shifted(latent, ko, -1)), device_id_type=MESH,
                ).start()
                return c

            lax.fori_loop(jnp.where(run == 0, 1, 0) if kd == 0 else 0, PEERS, one, 0)
            return carry

        lax.fori_loop(0, RUNS // 2, pack, 0)
        for part in range(PARTS):
            turned = lax.dot_general(
                unit, codes_rows[:, part * block : (part + 1) * block], (((1,), (1,)), ((), ())),
                preferred_element_type=F32,
            )
            codes_t[kd, part * block : (part + 1) * block, half * HALF * PAD : (half + 1) * HALF * PAD] = turned.astype(BF16)

    copies = []
    for half in range(2):
        first = 1 if half == 0 else HALF
        bytes_wait(codes_in.at[0, first : (half + 1) * HALF], code_recv.at[half])
        for kd in range(1, GROUPS):
            copy = pltpu.make_async_remote_copy(
                codes_in.at[0, pl.ds(half * HALF, HALF)], codes_in.at[kd, pl.ds(half * HALF, HALF)],
                copy_send.at[half, kd - 1], copy_recv.at[half, kd - 1],
                device_id=((dp + kd) % GROUPS, latent), device_id_type=MESH,
            )
            copy.start()
            copies.append((kd, half, copy))
        if half == 0:
            load_w.wait()
        forward(0, half)
    own_term = pltpu.make_async_copy(sent.at[0, 0], terms_in.at[0, 0], own_sem.at[1])
    own_term.start()
    for kd in range(1, GROUPS):
        for half in range(2):
            for ckd, chalf, copy in copies:
                if ckd == kd and chalf == half:
                    copy.wait_recv()
            forward(kd, half)
    own_term.wait()
    load_act.wait()

    stores = []
    for kd in range(GROUPS):
        first = 1 if kd == 0 else 0
        bytes_wait(terms_in.at[kd, first:OWNERS], term_recv.at[kd])

        def spread(run, carry):
            got = terms_in[kd, pl.ds(run * PEERS, PEERS)].reshape(PEERS * SENT, columns)
            flat = dot(spread_ref[...], got).astype(BF16)
            wide_tmp[:, pl.ds(run * BATCH, BATCH), :] = flat.reshape(PARTS, BATCH, columns)
            return carry

        lax.fori_loop(0, RUNS, spread, 0)
        slab = (dp + kd) % GROUPS

        def combine(part, carry):
            at = pl.ds(pl.multiple_of((slab * PARTS + part) * columns, columns), columns)
            wide = dot(take_ref[...], wide_tmp[part]) + bias_ref[:, at]
            rebuilt_ref[:, at] = wide.astype(BF16)
            error = (wide - act_ref[:, at].astype(F32)).astype(BF16)
            error_tmp[:, part] = dot(put_ref[...], error).astype(BF16).reshape(RUNS, BATCH, columns)
            return carry

        lax.fori_loop(0, PARTS, combine, 0)
        at = pl.ds(pl.multiple_of(slab * PARTS * columns, PARTS * columns), PARTS * columns)
        store = pltpu.make_async_copy(rebuilt_ref.at[:, at], rebuilt_hbm.at[:, at], rebuilt_sem.at[kd])
        store.start()
        stores.append(store)
        bytes_wait(sent.at[kd, first:OWNERS], term_send.at[kd])

        def pack(run, carry):
            message = dot(pack_ref[...], error_tmp[run].reshape(STACK, columns)).astype(BF16)
            sent[kd, pl.ds(run * PEERS, PEERS)] = message.reshape(PEERS, SENT, columns)

            def one(i, c):
                ko = run * PEERS + i
                pltpu.make_async_remote_copy(
                    sent.at[kd, ko], errors_in.at[kd, ko], error_send.at[kd], error_recv.at[kd],
                    device_id=((dp + kd) % GROUPS, shifted(latent, ko, 1)), device_id_type=MESH,
                ).start()
                return c

            lax.fori_loop(jnp.where(run == 0, 1, 0) if kd == 0 else 0, PEERS, one, 0)
            return carry

        lax.fori_loop(0, RUNS, pack, 0)
        if kd == 0:
            own_error = pltpu.make_async_copy(sent.at[0, 0], errors_in.at[0, 0], own_sem.at[2])
            own_error.start()
    own_error.wait()

    for kd in range(GROUPS):
        first = 1 if kd == 0 else 0
        bytes_wait(errors_in.at[kd, first:OWNERS], error_recv.at[kd])

        def spread(run, carry):
            got = errors_in[kd, pl.ds(run * PEERS, PEERS)].reshape(PEERS * SENT, columns)
            flat = dot(spread_ref[...], got).astype(BF16)
            for part in range(PARTS):
                error_rows[pl.ds(run * BATCH, BATCH), part * columns : (part + 1) * columns] = flat[
                    part * BATCH : (part + 1) * BATCH
                ]
            return carry

        lax.fori_loop(0, RUNS, spread, 0)
        if kd < GROUPS - 1:

            def accumulate(n, carry):
                at = pl.ds(pl.multiple_of(n * columns, columns), columns)
                more = dot(codes_t[kd], error_rows[:, at])
                total[:, at] = more if kd == 0 else total[:, at] + more
                return carry

            lax.fori_loop(0, PARTS, accumulate, 0)
        else:
            writes = []
            for n in range(PARTS):
                at = slice(n * columns, (n + 1) * columns)
                more = dot(codes_t[kd], error_rows[:, at])
                slot = n % stage.shape[0]
                if n >= stage.shape[0]:
                    writes[n - stage.shape[0]].wait()
                stage[slot] = ((total[:, at] + more) * loss_scale).astype(BF16)
                write = pltpu.make_async_copy(stage.at[slot], grad_hbm.at[:, at], stage_sem.at[slot])
                write.start()
                writes.append(write)
            for write in writes[-stage.shape[0] :]:
                write.wait()
    for store in stores:
        store.wait()
    bytes_wait(codes_out.at[1:OWNERS], code_send)
    for _, _, copy in copies:
        copy.wait_send()
    for kd in range(GROUPS):
        bytes_wait(sent.at[kd, (1 if kd == 0 else 0) : OWNERS], error_send.at[kd])


def on_device(activations, owner_ids, block_mask, latent_codes, w_dec, b_dec):
    rows, model_width = activations.shape
    slab, part_width = w_dec.shape
    block, columns = slab // PARTS, part_width // PARTS
    latent = lax.axis_index("latent")
    owner = owner_ids.T
    relative = (
        (owner // 16 - latent // 16) % 4 * 16 + (owner // 8 - latent // 8) % 2 * 8 + (owner - latent) % 8
    )
    order = message_order()
    vmem = pl.BlockSpec(memory_space=pltpu.VMEM)
    hbm = pl.BlockSpec(memory_space=pl.ANY)
    dma = pltpu.SemaphoreType.DMA
    return pl.pallas_call(
        kernel,
        out_shape=(
            jax.ShapeDtypeStruct((rows, model_width), BF16),
            jax.ShapeDtypeStruct((slab, part_width), BF16),
        ),
        in_specs=[vmem] * 6 + [hbm] * 2,
        out_specs=(hbm, hbm),
        scratch_shapes=[
            pltpu.VMEM((slab, part_width), BF16),
            pltpu.VMEM((rows, model_width), BF16),
            pltpu.VMEM((rows, model_width), BF16),
            pltpu.VMEM((rows, OWNERS * PAD), BF16),
            pltpu.VMEM((OWNERS * PAD, rows), BF16),
            pltpu.VMEM((OWNERS, SENT, block), BF16),
            pltpu.VMEM((GROUPS, OWNERS, SENT, block), BF16),
            pltpu.VMEM((GROUPS, slab, OWNERS * PAD), BF16),
            pltpu.VMEM((HALF * PAD, slab), BF16),
            pltpu.VMEM((RUNS, PARTS, BATCH, block), BF16),
            pltpu.VMEM((RUNS // 2, PARTS, BATCH, columns), BF16),
            pltpu.VMEM((GROUPS, OWNERS, SENT, columns), BF16),
            pltpu.VMEM((GROUPS, OWNERS, SENT, columns), BF16),
            pltpu.VMEM((GROUPS, OWNERS, SENT, columns), BF16),
            pltpu.VMEM((PARTS, OWNERS * PAD, columns), BF16),
            pltpu.VMEM((RUNS, PARTS, BATCH, columns), BF16),
            pltpu.VMEM((OWNERS * PAD, part_width), BF16),
            pltpu.VMEM((slab, part_width), F32),
            pltpu.VMEM((2, slab, columns), BF16),
            dma((2,)), dma((3,)), dma, dma((2,)), dma((2, GROUPS - 1)), dma((2, GROUPS - 1)),
            dma((GROUPS,)), dma((GROUPS,)), dma((GROUPS,)), dma((GROUPS,)), dma((GROUPS,)), dma((2,)),
        ],
        compiler_params=pltpu.CompilerParams(has_side_effects=True, vmem_limit_bytes=60 << 20),
        name="routed_decoder",
    )(
        (relative * PAD).astype(F32),
        block_mask.transpose(1, 2, 0),
        latent_codes.reshape(rows, 2 * slab),
        b_dec[None, :],
        jnp.asarray(order, BF16),
        jnp.asarray(order.T, BF16),
        activations,
        w_dec,
    )


def solution(mesh):
    placed = (
        P(("dp", "latent"), None),
        P(("dp", "latent"), None),
        P(("dp", "latent"), None, None),
        P(("dp", "latent"), None, None),
        P("latent", "dp"),
        P(),
    )
    return jax.shard_map(
        on_device,
        mesh=mesh,
        in_specs=placed,
        out_specs=(P(("dp", "latent"), None), P("latent", "dp")),
        check_vma=False,
    )
```

```python
import jax
import jax.numpy as jnp
import numpy as np
from jax import lax
from jax.experimental import pallas as pl
from jax.experimental.pallas import tpu as pltpu
from jax.sharding import PartitionSpec as P

loss_scale = 1.0 / 32.0
MOST = 6
PAD = 8
PEERS = 8
PARTS = 8
GROUPS = 4
OWNERS = 64
HALF = OWNERS // 2
RUNS = OWNERS // PEERS
BATCH = PEERS * PAD
STACK = PARTS * BATCH
SENT = PARTS * MOST
BF16, F32 = jnp.bfloat16, jnp.float32
MESH = pl.DeviceIdType.MESH


def message_order():
    out = np.zeros((PARTS, PEERS, PAD, PEERS, PARTS, MOST), np.float32)
    for part in range(PARTS):
        for peer in range(PEERS):
            for slot in range(MOST):
                out[part, peer, slot, peer, part, slot] = 1
    return out.reshape(STACK, PEERS * SENT)


def dot(a, b):
    return jnp.dot(a, b, preferred_element_type=F32)


def shifted(latent, offset, sign):
    y = (latent // 16 + sign * (offset // 16) + 4) % 4
    x = (latent // 8 + offset // 8) % 2
    z = (latent % 8 + sign * (offset % 8) + 8) % 8
    return y * 16 + x * 8 + z


def bytes_wait(ref, sem):
    pltpu.make_async_copy(ref, ref, sem).wait()


def kernel(
    rel_ref, mask_ref, codes_ref, bias_hbm, spread_hbm, pack_hbm, act_hbm, w_hbm,
    rebuilt_ref, grad_ref,
    w_ref, act_ref, bias_ref, spread_ref, pack_ref, take_ref, put_ref, place_ref, used_ref, codes_out, codes_in, codes_t, codes_rows,
    term_tmp, sent, terms_in, errors_in, wide_tmp, error_tmp, total,
    load_sem, code_send, code_recv, copy_send, copy_recv, term_send, term_recv, error_send, error_recv,
):
    dp = lax.axis_index("dp")
    latent = lax.axis_index("latent")
    rows = act_ref.shape[0]
    barrier = pltpu.get_barrier_semaphore()

    def greet(ko, carry):
        pl.semaphore_signal(barrier, inc=1, device_id=(dp, shifted(latent, ko, 1)), device_id_type=MESH)
        return carry

    lax.fori_loop(1, OWNERS, greet, 0)
    for kd in range(1, GROUPS):
        pl.semaphore_signal(barrier, inc=1, device_id=((dp + kd) % GROUPS, latent), device_id_type=MESH)
    load_w = pltpu.make_async_copy(w_hbm, w_ref, load_sem.at[0])
    load_act = pltpu.make_async_copy(act_hbm, act_ref, load_sem.at[1])
    load_pack = pltpu.make_async_copy(pack_hbm, pack_ref, load_sem.at[2])
    load_spread = pltpu.make_async_copy(spread_hbm, spread_ref, load_sem.at[3])
    load_bias = pltpu.make_async_copy(bias_hbm, bias_ref, load_sem.at[4])
    load_pack.start()
    load_spread.start()
    load_w.start()
    load_bias.start()
    load_act.start()

    down = lax.broadcasted_iota(jnp.int32, (rows, rows), 0)
    across = lax.broadcasted_iota(jnp.int32, (rows, rows), 1)
    along = [jnp.broadcast_to(rel_ref[g : g + 1, :], (rows, rows)) for g in range(2)]
    below = [jnp.transpose(a) for a in along]
    slot_row = lax.broadcasted_iota(jnp.int32, (OWNERS * PAD, rows), 0).astype(F32)
    puts = []
    for g in range(2):
        count = [jnp.where(below[o] == along[g], 1.0, 0.0) for o in range(2)]
        here = rel_ref[g : g + 1, :] + jnp.sum(jnp.where(down < across, count[0] + count[1], 0.0), axis=0, keepdims=True)
        puts.append(jnp.where(slot_row == here, 1.0, 0.0))
    place_ref[...] = jnp.concatenate(puts, axis=1).astype(BF16)
    width = codes_ref.shape[1] // 2
    block = width // PARTS
    live = jnp.concatenate([mask_ref[...].astype(F32), jnp.zeros((rows - 2 * PARTS, rows), F32)], axis=0)
    live = jnp.transpose(live)
    for g in range(2):
        for part in range(PARTS):
            at = slice(part * block, (part + 1) * block)
            codes = codes_ref[:, g * width + part * block : g * width + (part + 1) * block].astype(F32)
            column = g * PARTS + part
            used_ref[g * rows : (g + 1) * rows, at] = (codes * live[:, column : column + 1]).astype(BF16)
    load_pack.wait()
    pl.semaphore_wait(barrier, OWNERS - 1 + GROUPS - 1)

    def send_codes(run, carry):
        placed = dot(place_ref[pl.ds(run * BATCH, BATCH), :], used_ref[...]).astype(BF16)
        stacked = jnp.concatenate([placed[:, part * block : (part + 1) * block] for part in range(PARTS)], axis=0)
        message = dot(pack_ref[...], stacked).astype(BF16)
        codes_out[pl.ds(run * PEERS, PEERS)] = message.reshape(PEERS, SENT, block)

        def one(i, c):
            ko = run * PEERS + i
            pltpu.make_async_remote_copy(
                codes_out.at[ko], codes_in.at[0, ko], code_send, code_recv.at[run // (RUNS // 2)],
                device_id=(dp, shifted(latent, ko, 1)), device_id_type=MESH,
            ).start()
            return c

        lax.fori_loop(jnp.where(run == 0, 1, 0), PEERS, one, 0)
        return carry

    lax.fori_loop(0, RUNS, send_codes, 0)
    pltpu.make_async_copy(codes_out.at[0], codes_in.at[0, 0], code_recv.at[0]).start()
    put_ref[...] = (puts[0] + puts[1]).astype(BF16)
    slot_lane = lax.broadcasted_iota(jnp.int32, (rows, OWNERS * PAD), 1).astype(F32)
    take = jnp.zeros((rows, OWNERS * PAD), F32)
    for g in range(2):
        count = [jnp.where(below[g] == along[o], 1.0, 0.0) for o in range(2)]
        here = below[g][:, :1] + jnp.sum(jnp.where(across < down, count[0] + count[1], 0.0), axis=1, keepdims=True)
        take = take + jnp.where(slot_lane == here, 1.0, 0.0)
    take_ref[...] = take.astype(BF16)
    unit = lax.broadcasted_iota(jnp.int32, (block, block), 0) == lax.broadcasted_iota(jnp.int32, (block, block), 1)
    unit = jnp.where(unit, 1.0, 0.0).astype(BF16)
    columns = w_ref.shape[1] // PARTS

    def forward(kd, half):
        def spread(g, carry):
            got = codes_in[kd, pl.ds(half * HALF + g * PEERS, PEERS)].reshape(PEERS * SENT, block)
            flat = dot(spread_ref[...], got).astype(BF16)
            for part in range(PARTS):
                codes_rows[pl.ds(g * BATCH, BATCH), part * block : (part + 1) * block] = flat[
                    part * BATCH : (part + 1) * BATCH
                ]
            return carry

        lax.fori_loop(0, RUNS // 2, spread, 0)

        def decode(n, carry):
            at = pl.ds(pl.multiple_of(n * columns, columns), columns)
            term = dot(codes_rows[...], w_ref[:, at]).astype(BF16)
            term_tmp[:, n] = term.reshape(RUNS // 2, BATCH, columns)
            return carry

        lax.fori_loop(0, PARTS, decode, 0)

        def pack(g, carry):
            run = half * (RUNS // 2) + g
            message = dot(pack_ref[...], term_tmp[g].reshape(STACK, columns)).astype(BF16)
            sent[kd, pl.ds(run * PEERS, PEERS)] = message.reshape(PEERS, SENT, columns)

            def one(i, c):
                ko = run * PEERS + i
                pltpu.make_async_remote_copy(
                    sent.at[kd, ko], terms_in.at[kd, ko], term_send.at[kd], term_recv.at[kd, run],
                    device_id=((dp - kd + GROUPS) % GROUPS, shifted(latent, ko, -1)), device_id_type=MESH,
                ).start()
                return c

            lax.fori_loop(jnp.where(run == 0, 1, 0) if kd == 0 else 0, PEERS, one, 0)
            return carry

        lax.fori_loop(0, RUNS // 2, pack, 0)
        for part in range(PARTS):
            turned = lax.dot_general(
                unit, codes_rows[:, part * block : (part + 1) * block], (((1,), (1,)), ((), ())),
                preferred_element_type=F32,
            )
            codes_t[kd, part * block : (part + 1) * block, half * HALF * PAD : (half + 1) * HALF * PAD] = turned.astype(BF16)

    copies = []
    for half in range(2):
        bytes_wait(codes_in.at[0, pl.ds(half * HALF, HALF)], code_recv.at[half])
        for kd in range(1, GROUPS):
            copy = pltpu.make_async_remote_copy(
                codes_in.at[0, pl.ds(half * HALF, HALF)], codes_in.at[kd, pl.ds(half * HALF, HALF)],
                copy_send.at[half, kd - 1], copy_recv.at[half, kd - 1],
                device_id=((dp + kd) % GROUPS, latent), device_id_type=MESH,
            )
            copy.start()
            copies.append((kd, half, copy))
        if half == 0:
            load_spread.wait()
            load_w.wait()
        forward(0, half)
    pltpu.make_async_copy(sent.at[0, 0], terms_in.at[0, 0], term_recv.at[0, 0]).start()
    for kd in range(1, GROUPS):
        for half in range(2):
            for ckd, chalf, copy in copies:
                if ckd == kd and chalf == half:
                    copy.wait_recv()
            forward(kd, half)
    load_act.wait()
    load_bias.wait()

    for kd in range(GROUPS):

        def spread(run, carry):
            bytes_wait(terms_in.at[kd, pl.ds(run * PEERS, PEERS)], term_recv.at[kd, run])
            got = terms_in[kd, pl.ds(run * PEERS, PEERS)].reshape(PEERS * SENT, columns)
            flat = dot(spread_ref[...], got).astype(BF16)
            wide_tmp[:, pl.ds(run * BATCH, BATCH), :] = flat.reshape(PARTS, BATCH, columns)
            return carry

        lax.fori_loop(0, RUNS, spread, 0)
        slab = (dp + kd) % GROUPS

        def combine(part, carry):
            at = pl.ds(pl.multiple_of((slab * PARTS + part) * columns, columns), columns)
            wide = dot(take_ref[...], wide_tmp[part]) + bias_ref[:, at]
            rebuilt_ref[:, at] = wide.astype(BF16)
            error = (wide - act_ref[:, at].astype(F32)).astype(BF16)
            error_tmp[:, part] = dot(put_ref[...], error).astype(BF16).reshape(RUNS, BATCH, columns)
            return carry

        lax.fori_loop(0, PARTS, combine, 0)
        bytes_wait(sent.at[kd, (1 if kd == 0 else 0) : OWNERS], term_send.at[kd])

        def pack(run, carry):
            message = dot(pack_ref[...], error_tmp[run].reshape(STACK, columns)).astype(BF16)
            sent[kd, pl.ds(run * PEERS, PEERS)] = message.reshape(PEERS, SENT, columns)

            def one(i, c):
                ko = run * PEERS + i
                pltpu.make_async_remote_copy(
                    sent.at[kd, ko], errors_in.at[kd, ko], error_send.at[kd], error_recv.at[kd, run],
                    device_id=((dp + kd) % GROUPS, shifted(latent, ko, 1)), device_id_type=MESH,
                ).start()
                return c

            lax.fori_loop(jnp.where(run == 0, 1, 0) if kd == 0 else 0, PEERS, one, 0)
            return carry

        lax.fori_loop(0, RUNS, pack, 0)
        if kd == 0:
            pltpu.make_async_copy(sent.at[0, 0], errors_in.at[0, 0], error_recv.at[0, 0]).start()

    for kd in range(GROUPS):
        for half in range(2):

            def spread(g, carry):
                run = half * (RUNS // 2) + g
                bytes_wait(errors_in.at[kd, pl.ds(run * PEERS, PEERS)], error_recv.at[kd, run])
                got = errors_in[kd, pl.ds(run * PEERS, PEERS)].reshape(PEERS * SENT, columns)
                flat = dot(spread_ref[...], got).astype(BF16)
                wide_tmp[:, pl.ds(g * BATCH, BATCH), :] = flat.reshape(PARTS, BATCH, columns)
                return carry

            lax.fori_loop(0, RUNS // 2, spread, 0)

            def accumulate(n, carry):
                at = pl.ds(pl.multiple_of(n * columns, columns), columns)
                codes = codes_t[kd, :, half * HALF * PAD : (half + 1) * HALF * PAD]
                more = dot(codes, wide_tmp[n, : HALF * PAD, :])
                if (kd, half) == (0, 0):
                    total[:, at] = more
                elif (kd, half) == (GROUPS - 1, 1):
                    grad_ref[:, at] = ((total[:, at] + more) * loss_scale).astype(BF16)
                else:
                    total[:, at] = total[:, at] + more
                return carry

            lax.fori_loop(0, PARTS, accumulate, 0)
    bytes_wait(codes_out.at[1:OWNERS], code_send)
    for _, _, copy in copies:
        copy.wait_send()
    for kd in range(GROUPS):
        bytes_wait(sent.at[kd, (1 if kd == 0 else 0) : OWNERS], error_send.at[kd])


def on_device(activations, owner_ids, block_mask, latent_codes, w_dec, b_dec):
    rows, model_width = activations.shape
    slab, part_width = w_dec.shape
    block, columns = slab // PARTS, part_width // PARTS
    latent = lax.axis_index("latent")
    owner = owner_ids.T
    relative = (
        (owner // 16 - latent // 16) % 4 * 16 + (owner // 8 - latent // 8) % 2 * 8 + (owner - latent) % 8
    )
    order = message_order()
    vmem = pl.BlockSpec(memory_space=pltpu.VMEM)
    hbm = pl.BlockSpec(memory_space=pl.ANY)
    dma = pltpu.SemaphoreType.DMA
    return pl.pallas_call(
        kernel,
        out_shape=(
            pltpu.VMEM((rows, model_width), BF16),
            pltpu.VMEM((slab, part_width), BF16),
        ),
        in_specs=[vmem] * 3 + [hbm] * 5,
        out_specs=(vmem, vmem),
        scratch_shapes=[
            pltpu.VMEM((slab, part_width), BF16),
            pltpu.VMEM((rows, model_width), BF16),
            pltpu.VMEM((1, model_width), F32),
            pltpu.VMEM((STACK, PEERS * SENT), BF16),
            pltpu.VMEM((PEERS * SENT, STACK), BF16),
            pltpu.VMEM((rows, OWNERS * PAD), BF16),
            pltpu.VMEM((OWNERS * PAD, rows), BF16),
            pltpu.VMEM((OWNERS * PAD, 2 * rows), BF16),
            pltpu.VMEM((2 * rows, slab), BF16),
            pltpu.VMEM((OWNERS, SENT, block), BF16),
            pltpu.VMEM((GROUPS, OWNERS, SENT, block), BF16),
            pltpu.VMEM((GROUPS, slab, OWNERS * PAD), BF16),
            pltpu.VMEM((HALF * PAD, slab), BF16),
            pltpu.VMEM((RUNS // 2, PARTS, BATCH, columns), BF16),
            pltpu.VMEM((GROUPS, OWNERS, SENT, columns), BF16),
            pltpu.VMEM((GROUPS, OWNERS, SENT, columns), BF16),
            pltpu.VMEM((GROUPS, OWNERS, SENT, columns), BF16),
            pltpu.VMEM((PARTS, OWNERS * PAD, columns), BF16),
            pltpu.VMEM((RUNS, PARTS, BATCH, columns), BF16),
            pltpu.VMEM((slab, part_width), F32),
            dma((5,)), dma, dma((2,)), dma((2, GROUPS - 1)), dma((2, GROUPS - 1)),
            dma((GROUPS,)), dma((GROUPS, RUNS)), dma((GROUPS,)), dma((GROUPS, RUNS)),
        ],
        compiler_params=pltpu.CompilerParams(has_side_effects=True, collective_id=0, vmem_limit_bytes=50 << 20),
        name="routed_decoder",
    )(
        (relative * PAD).astype(F32),
        block_mask.transpose(1, 2, 0).reshape(2 * PARTS, rows),
        pltpu.with_memory_space_constraint(latent_codes.reshape(rows, 2 * slab), pltpu.VMEM),
        b_dec[None, :],
        jnp.asarray(order, BF16),
        jnp.asarray(order.T, BF16),
        activations,
        w_dec,
    )


def solution(mesh):
    placed = (
        P(("dp", "latent"), None),
        P(("dp", "latent"), None),
        P(("dp", "latent"), None, None),
        P(("dp", "latent"), None, None),
        P("latent", "dp"),
        P(),
    )
    return jax.shard_map(
        on_device,
        mesh=mesh,
        in_specs=placed,
        out_specs=(P(("dp", "latent"), None), P("latent", "dp")),
        check_vma=False,
    )
```

```python
import jax
import jax.numpy as jnp
import numpy as np
from jax import lax
from jax.experimental import pallas as pl
from jax.experimental.pallas import tpu as pltpu
from jax.sharding import PartitionSpec as P

loss_scale = 1.0 / 32.0
MOST = 6
PAD = 8
PEERS = 8
PARTS = 8
GROUPS = 4
OWNERS = 64
HALF = OWNERS // 2
RUNS = OWNERS // PEERS
BATCH = PEERS * PAD
STACK = PARTS * BATCH
SENT = PARTS * MOST
BF16, F32 = jnp.bfloat16, jnp.float32
MESH = pl.DeviceIdType.MESH


def message_order():
    out = np.zeros((PARTS, PEERS, PAD, PEERS, PARTS, MOST), np.float32)
    for part in range(PARTS):
        for peer in range(PEERS):
            for slot in range(MOST):
                out[part, peer, slot, peer, part, slot] = 1
    return out.reshape(STACK, PEERS * SENT)


def dot(a, b):
    return jnp.dot(a, b, preferred_element_type=F32)


def shifted(latent, offset, sign):
    y = (latent // 16 + sign * (offset // 16) + 4) % 4
    x = (latent // 8 + offset // 8) % 2
    z = (latent % 8 + sign * (offset % 8) + 8) % 8
    return y * 16 + x * 8 + z


def relay_step(z_offset, y_offset):
    ahead = jnp.where(z_offset + y_offset % 2 <= 4, 1, -1)
    return jnp.where(z_offset == 0, 0, ahead)


def relayed(latent, offset, sign):
    y = (latent // 16 + sign * (offset // 16) + 4) % 4
    x = (latent // 8 + offset // 8) % 2
    z = (latent % 8 + sign * (offset % 8 - relay_step(offset % 8, offset // 16)) + 16) % 8
    return y * 16 + x * 8 + z


def relay_roles(rows):
    out = np.zeros((OWNERS, PAD, rows), np.float32)
    for offset in range(OWNERS):
        if offset % 8:
            out[offset] = 1 if offset % 8 + offset // 16 % 2 <= 4 else 2
    return out.reshape(OWNERS * PAD, rows)


def bytes_wait(ref, sem):
    pltpu.make_async_copy(ref, ref, sem).wait()


def kernel(
    rel_ref, mask_ref, codes_ref, bias_hbm, spread_hbm, pack_hbm, roles_hbm, act_hbm, w_hbm,
    rebuilt_ref, grad_ref,
    w_ref, act_ref, bias_ref, spread_ref, pack_ref, roles_ref, take_ref, put_ref, place_ref, used_ref, codes_out, codes_in, codes_t, codes_rows,
    slot_out, slot_in, error_all, sent, terms_in, errors_in, wide_tmp, error_tmp, total,
    load_sem, code_send, code_recv, copy_send, copy_recv, term_send, term_recv, error_send, error_recv,
    slot_send, slot_recv, row_send, row_recv,
):
    dp = lax.axis_index("dp")
    latent = lax.axis_index("latent")
    rows = act_ref.shape[0]
    barrier = pltpu.get_barrier_semaphore()

    def greet(ko, carry):
        pl.semaphore_signal(barrier, inc=1, device_id=(dp, shifted(latent, ko, 1)), device_id_type=MESH)
        return carry

    lax.fori_loop(1, OWNERS, greet, 0)
    for kd in range(1, GROUPS):
        pl.semaphore_signal(barrier, inc=1, device_id=((dp + kd) % GROUPS, latent), device_id_type=MESH)
    load_w = pltpu.make_async_copy(w_hbm, w_ref, load_sem.at[0])
    load_act = pltpu.make_async_copy(act_hbm, act_ref, load_sem.at[1])
    load_pack = pltpu.make_async_copy(pack_hbm, pack_ref, load_sem.at[2])
    load_spread = pltpu.make_async_copy(spread_hbm, spread_ref, load_sem.at[3])
    load_bias = pltpu.make_async_copy(bias_hbm, bias_ref, load_sem.at[4])
    load_roles = pltpu.make_async_copy(roles_hbm, roles_ref, load_sem.at[5])
    load_pack.start()
    load_roles.start()
    load_spread.start()
    load_w.start()
    load_bias.start()
    load_act.start()

    down = lax.broadcasted_iota(jnp.int32, (rows, rows), 0)
    across = lax.broadcasted_iota(jnp.int32, (rows, rows), 1)
    along = [jnp.broadcast_to(rel_ref[g : g + 1, :], (rows, rows)) for g in range(2)]
    below = [jnp.transpose(a) for a in along]
    slot_row = lax.broadcasted_iota(jnp.int32, (OWNERS * PAD, rows), 0).astype(F32)
    slot_out[...] = jnp.zeros_like(slot_out)
    puts = []
    for g in range(2):
        count = [jnp.where(below[o] == along[g], 1.0, 0.0) for o in range(2)]
        here = rel_ref[g : g + 1, :] + jnp.sum(jnp.where(down < across, count[0] + count[1], 0.0), axis=0, keepdims=True)
        slot_out[g : g + 1, :] = here
        puts.append(jnp.where(slot_row == here, 1.0, 0.0))
    place_ref[...] = jnp.concatenate(puts, axis=1).astype(BF16)
    width = codes_ref.shape[1] // 2
    block = width // PARTS
    live = jnp.concatenate([mask_ref[...].astype(F32), jnp.zeros((rows - 2 * PARTS, rows), F32)], axis=0)
    live = jnp.transpose(live)
    for g in range(2):
        for part in range(PARTS):
            at = slice(part * block, (part + 1) * block)
            codes = codes_ref[:, g * width + part * block : g * width + (part + 1) * block].astype(F32)
            column = g * PARTS + part
            used_ref[g * rows : (g + 1) * rows, at] = (codes * live[:, column : column + 1]).astype(BF16)
    load_pack.wait()
    pl.semaphore_wait(barrier, OWNERS - 1 + GROUPS - 1)
    beside = [(dp, shifted(latent, 1, -1)), (dp, shifted(latent, 1, 1))]

    def to_side(side, source, target, send, recv):
        return pltpu.make_async_remote_copy(
            source, target, send, recv, device_id=beside[side], device_id_type=MESH
        )

    slot_copies = [to_side(i, slot_out, slot_in.at[1 - i], slot_send.at[i], slot_recv.at[1 - i]) for i in range(2)]
    for copy in slot_copies:
        copy.start()

    def send_codes(run, carry):
        placed = dot(place_ref[pl.ds(run * BATCH, BATCH), :], used_ref[...]).astype(BF16)
        stacked = jnp.concatenate([placed[:, part * block : (part + 1) * block] for part in range(PARTS)], axis=0)
        message = dot(pack_ref[...], stacked).astype(BF16)
        codes_out[pl.ds(run * PEERS, PEERS)] = message.reshape(PEERS, SENT, block)

        def one(i, c):
            ko = run * PEERS + i
            pltpu.make_async_remote_copy(
                codes_out.at[ko], codes_in.at[0, ko], code_send, code_recv.at[run // (RUNS // 2)],
                device_id=(dp, shifted(latent, ko, 1)), device_id_type=MESH,
            ).start()
            return c

        lax.fori_loop(jnp.where(run == 0, 1, 0), PEERS, one, 0)
        return carry

    lax.fori_loop(0, RUNS, send_codes, 0)
    pltpu.make_async_copy(codes_out.at[0], codes_in.at[0, 0], code_recv.at[0]).start()
    load_roles.wait()
    for role in range(3):
        if role:
            bytes_wait(slot_in.at[role - 1], slot_recv.at[role - 1])
        put = jnp.zeros((OWNERS * PAD, rows), F32)
        for g in range(2):
            where = slot_in[role - 1, g : g + 1, :] if role else slot_out[g : g + 1, :]
            put = put + jnp.where(slot_row == where, 1.0, 0.0)
        if role == 0:
            take_ref[...] = jnp.transpose(put).astype(BF16)
        put = jnp.where(roles_ref[...] == float(role), put, 0.0)
        put_ref[:, role * rows : (role + 1) * rows] = put.astype(BF16)
    unit = lax.broadcasted_iota(jnp.int32, (block, block), 0) == lax.broadcasted_iota(jnp.int32, (block, block), 1)
    unit = jnp.where(unit, 1.0, 0.0).astype(BF16)
    columns = w_ref.shape[1] // PARTS

    def forward(kd, half):
        def spread(g, carry):
            got = codes_in[kd, pl.ds(half * HALF + g * PEERS, PEERS)].reshape(PEERS * SENT, block)
            flat = dot(spread_ref[...], got).astype(BF16)
            for part in range(PARTS):
                codes_rows[pl.ds(g * BATCH, BATCH), part * block : (part + 1) * block] = flat[
                    part * BATCH : (part + 1) * BATCH
                ]
            return carry

        lax.fori_loop(0, RUNS // 2, spread, 0)

        def decode(n, carry):
            at = pl.ds(pl.multiple_of(n * columns, columns), columns)
            term = dot(codes_rows[...], w_ref[:, at]).astype(BF16)
            error_tmp[: RUNS // 2, n] = term.reshape(RUNS // 2, BATCH, columns)
            return carry

        lax.fori_loop(0, PARTS, decode, 0)

        def pack(g, carry):
            run = half * (RUNS // 2) + g
            message = dot(pack_ref[...], error_tmp[g].reshape(STACK, columns)).astype(BF16)
            sent[kd, pl.ds(run * PEERS, PEERS)] = message.reshape(PEERS, SENT, columns)

            def one(i, c):
                ko = run * PEERS + i
                pltpu.make_async_remote_copy(
                    sent.at[kd, ko], terms_in.at[kd, ko], term_send.at[kd], term_recv.at[kd, run],
                    device_id=((dp - kd + GROUPS) % GROUPS, shifted(latent, ko, -1)), device_id_type=MESH,
                ).start()
                return c

            lax.fori_loop(jnp.where(run == 0, 1, 0) if kd == 0 else 0, PEERS, one, 0)
            return carry

        lax.fori_loop(0, RUNS // 2, pack, 0)
        for part in range(PARTS):
            turned = lax.dot_general(
                unit, codes_rows[:, part * block : (part + 1) * block], (((1,), (1,)), ((), ())),
                preferred_element_type=F32,
            )
            codes_t[kd, part * block : (part + 1) * block, half * HALF * PAD : (half + 1) * HALF * PAD] = turned.astype(BF16)

    copies = []
    for half in range(2):
        bytes_wait(codes_in.at[0, pl.ds(half * HALF, HALF)], code_recv.at[half])
        for kd in range(1, GROUPS):
            copy = pltpu.make_async_remote_copy(
                codes_in.at[0, pl.ds(half * HALF, HALF)], codes_in.at[kd, pl.ds(half * HALF, HALF)],
                copy_send.at[half, kd - 1], copy_recv.at[half, kd - 1],
                device_id=((dp + kd) % GROUPS, latent), device_id_type=MESH,
            )
            copy.start()
            copies.append((kd, half, copy))
        if half == 0:
            load_spread.wait()
            load_w.wait()
        forward(0, half)
    pltpu.make_async_copy(sent.at[0, 0], terms_in.at[0, 0], term_recv.at[0, 0]).start()

    def decode_for(kd):
        for half in range(2):
            for ckd, chalf, copy in copies:
                if ckd == kd and chalf == half:
                    copy.wait_recv()
            forward(kd, half)

    for kd in range(1, GROUPS):
        decode_for(kd)
    load_act.wait()
    load_bias.wait()

    def compare(kd):
        def spread(run, carry):
            bytes_wait(terms_in.at[kd, pl.ds(run * PEERS, PEERS)], term_recv.at[kd, run])
            got = terms_in[kd, pl.ds(run * PEERS, PEERS)].reshape(PEERS * SENT, columns)
            flat = dot(spread_ref[...], got).astype(BF16)
            wide_tmp[:, pl.ds(run * BATCH, BATCH), :] = flat.reshape(PARTS, BATCH, columns)
            return carry

        lax.fori_loop(0, RUNS, spread, 0)
        slab = (dp + kd) % GROUPS

        def combine(part, carry):
            at = pl.ds(pl.multiple_of((slab * PARTS + part) * columns, columns), columns)
            wide = dot(take_ref[...], wide_tmp[part]) + bias_ref[:, at]
            rebuilt_ref[:, at] = wide.astype(BF16)
            error_all[kd, part, :rows] = (wide - act_ref[:, at].astype(F32)).astype(BF16)
            for side in range(2):
                first = (2 - side) * rows
                to_side(
                    side, error_all.at[kd, part, :rows], error_all.at[kd, part, first : first + rows],
                    row_send.at[kd, side], row_recv.at[kd, 1 - side],
                ).start()
            return carry

        lax.fori_loop(0, PARTS, combine, 0)

    def scatter(kd):
        for side in range(2):
            first = (1 + side) * rows
            bytes_wait(error_all.at[kd, :, first : first + rows], row_recv.at[kd, side])

        def place(part, carry):
            placed = dot(put_ref[...], error_all[kd, part]).astype(BF16)
            error_tmp[:, part] = placed.reshape(RUNS, BATCH, columns)
            return carry

        lax.fori_loop(0, PARTS, place, 0)
        bytes_wait(sent.at[kd, (1 if kd == 0 else 0) : OWNERS], term_send.at[kd])

        def pack(run, carry):
            message = dot(pack_ref[...], error_tmp[run].reshape(STACK, columns)).astype(BF16)
            sent[kd, pl.ds(run * PEERS, PEERS)] = message.reshape(PEERS, SENT, columns)

            def one(i, c):
                ko = run * PEERS + i
                pltpu.make_async_remote_copy(
                    sent.at[kd, ko], errors_in.at[kd, ko], error_send.at[kd], error_recv.at[kd, run],
                    device_id=((dp + kd) % GROUPS, relayed(latent, ko, 1)), device_id_type=MESH,
                ).start()
                return c

            bounds = (jnp.where(run == 0, 2, 0), jnp.where(run == 0, PEERS - 1, PEERS)) if kd == 0 else (0, PEERS)
            lax.fori_loop(*bounds, one, 0)
            return carry

        lax.fori_loop(0, RUNS, pack, 0)
        if kd == 0:
            for ko in (0, 1, PEERS - 1):
                pltpu.make_async_copy(sent.at[0, ko], errors_in.at[0, ko], error_recv.at[0, 0]).start()

    compare(0)
    for kd in range(GROUPS):
        if kd < GROUPS - 1:
            compare(kd + 1)
        scatter(kd)

    for kd in range(GROUPS):
        for half in range(2):

            def spread(g, carry):
                run = half * (RUNS // 2) + g
                bytes_wait(errors_in.at[kd, pl.ds(run * PEERS, PEERS)], error_recv.at[kd, run])
                got = errors_in[kd, pl.ds(run * PEERS, PEERS)].reshape(PEERS * SENT, columns)
                flat = dot(spread_ref[...], got).astype(BF16)
                wide_tmp[:, pl.ds(g * BATCH, BATCH), :] = flat.reshape(PARTS, BATCH, columns)
                return carry

            lax.fori_loop(0, RUNS // 2, spread, 0)

            def accumulate(n, carry):
                at = pl.ds(pl.multiple_of(n * columns, columns), columns)
                codes = codes_t[kd, :, half * HALF * PAD : (half + 1) * HALF * PAD]
                more = dot(codes, wide_tmp[n, : HALF * PAD, :])
                if (kd, half) == (0, 0):
                    total[:, at] = more
                elif (kd, half) == (GROUPS - 1, 1):
                    grad_ref[:, at] = ((total[:, at] + more) * loss_scale).astype(BF16)
                else:
                    total[:, at] = total[:, at] + more
                return carry

            lax.fori_loop(0, PARTS, accumulate, 0)
    bytes_wait(codes_out.at[1:OWNERS], code_send)
    for _, _, copy in copies:
        copy.wait_send()
    for kd in range(GROUPS):
        bytes_wait(sent.at[kd, (3 if kd == 0 else 0) : OWNERS], error_send.at[kd])
    for copy in slot_copies:
        copy.wait_send()
    for kd in range(GROUPS):
        for side in range(2):
            bytes_wait(error_all.at[kd, :, :rows], row_send.at[kd, side])


def on_device(activations, owner_ids, block_mask, latent_codes, w_dec, b_dec):
    rows, model_width = activations.shape
    slab, part_width = w_dec.shape
    block, columns = slab // PARTS, part_width // PARTS
    latent = lax.axis_index("latent")
    owner = owner_ids.T
    relative = (
        (owner // 16 - latent // 16) % 4 * 16 + (owner // 8 - latent // 8) % 2 * 8 + (owner - latent) % 8
    )
    order = message_order()
    vmem = pl.BlockSpec(memory_space=pltpu.VMEM)
    hbm = pl.BlockSpec(memory_space=pl.ANY)
    dma = pltpu.SemaphoreType.DMA
    return pl.pallas_call(
        kernel,
        out_shape=(
            pltpu.VMEM((rows, model_width), BF16),
            pltpu.VMEM((slab, part_width), BF16),
        ),
        in_specs=[vmem] * 3 + [hbm] * 6,
        out_specs=(vmem, vmem),
        scratch_shapes=[
            pltpu.VMEM((slab, part_width), BF16),
            pltpu.VMEM((rows, model_width), BF16),
            pltpu.VMEM((1, model_width), F32),
            pltpu.VMEM((STACK, PEERS * SENT), BF16),
            pltpu.VMEM((PEERS * SENT, STACK), BF16),
            pltpu.VMEM((OWNERS * PAD, rows), F32),
            pltpu.VMEM((rows, OWNERS * PAD), BF16),
            pltpu.VMEM((OWNERS * PAD, 3 * rows), BF16),
            pltpu.VMEM((OWNERS * PAD, 2 * rows), BF16),
            pltpu.VMEM((2 * rows, slab), BF16),
            pltpu.VMEM((OWNERS, SENT, block), BF16),
            pltpu.VMEM((GROUPS, OWNERS, SENT, block), BF16),
            pltpu.VMEM((GROUPS, slab, OWNERS * PAD), BF16),
            pltpu.VMEM((HALF * PAD, slab), BF16),
            pltpu.VMEM((8, rows), F32),
            pltpu.VMEM((2, 8, rows), F32),
            pltpu.VMEM((GROUPS, PARTS, 3 * rows, columns), BF16),
            pltpu.VMEM((GROUPS, OWNERS, SENT, columns), BF16),
            pltpu.VMEM((GROUPS, OWNERS, SENT, columns), BF16),
            pltpu.VMEM((GROUPS, OWNERS, SENT, columns), BF16),
            pltpu.VMEM((PARTS, OWNERS * PAD, columns), BF16),
            pltpu.VMEM((RUNS, PARTS, BATCH, columns), BF16),
            pltpu.VMEM((slab, part_width), F32),
            dma((6,)), dma, dma((2,)), dma((2, GROUPS - 1)), dma((2, GROUPS - 1)),
            dma((GROUPS,)), dma((GROUPS, RUNS)), dma((GROUPS,)), dma((GROUPS, RUNS)),
            dma((2,)), dma((2,)), dma((GROUPS, 2)), dma((GROUPS, 2)),
        ],
        compiler_params=pltpu.CompilerParams(has_side_effects=True, collective_id=0, vmem_limit_bytes=57 << 20),
        name="routed_decoder",
    )(
        (relative * PAD).astype(F32),
        block_mask.transpose(1, 2, 0).reshape(2 * PARTS, rows),
        pltpu.with_memory_space_constraint(latent_codes.reshape(rows, 2 * slab), pltpu.VMEM),
        b_dec[None, :],
        jnp.asarray(order, BF16),
        jnp.asarray(order.T, BF16),
        jnp.asarray(relay_roles(rows)),
        activations,
        w_dec,
    )


def solution(mesh):
    placed = (
        P(("dp", "latent"), None),
        P(("dp", "latent"), None),
        P(("dp", "latent"), None, None),
        P(("dp", "latent"), None, None),
        P("latent", "dp"),
        P(),
    )
    return jax.shard_map(
        on_device,
        mesh=mesh,
        in_specs=placed,
        out_specs=(P(("dp", "latent"), None), P("latent", "dp")),
        check_vma=False,
    )
```
